32 devices in a mesh: dp: 16 (over z, y, core), mp: 2 (over x).
Axes of the slice: x: 2, y: 2, z: 4, core: 2. Of those that a mesh axis runs over, the one named last changes fastest.
Arguments:
- activations: bfloat16 [8192, 28672], P('dp', 'mp'), may hold values from -200 to 200
- weight: bfloat16 [8192, 28672], P(None, ('mp', 'dp')), may hold values from -25 to 25
- thresholds: float32 [8192], P('dp'), may hold values from 0.5 to 1.5
Outputs:
- pruned: bfloat16 [8192, 28672], P('dp', 'mp')
The draws below stay inside these ranges and needn't reach their ends.
All inputs are finite; a program needn't handle non-finite values.
Results may differ from the reference program's by a relative error of at most 0.0004.
Values may be sent and summed in bfloat16 or wider, within the bound.
No kernel may reach another device: no remote copies, remote signals or barrier semaphores. Data moves between devices by JAX's collectives and lax.ppermute only.
A program may use at most 128 MiB of HBM per device.

```python
import jax
import jax.numpy as jnp
from jax import lax

OUT = 8192
IN = 28672
TOKENS = 8192
N_DP = 16


def draw_activations(key, part):
    keys = jax.random.split(jax.random.fold_in(key, 11), 3)
    positions = jnp.arange(TOKENS, dtype=jnp.float32)[:, None]
    row_scale = 10.0 ** jax.random.uniform(keys[0], (TOKENS, 1), jnp.float32) * 3.0 ** (positions / TOKENS - 1.0)
    col_scale = 10.0 ** (jax.random.uniform(keys[1], (1, IN), jnp.float32) - 0.5)
    noise = jnp.clip(jax.random.normal(keys[2], (TOKENS, IN), jnp.float32), -4.0, 4.0)
    return (noise * row_scale * col_scale).astype(jnp.bfloat16)


def draw_weight(key, part):
    keys = jax.random.split(jax.random.fold_in(key, 23), 2)
    columns = jnp.arange(IN, dtype=jnp.float32)[None, :]
    col_scale = 10.0 ** (jax.random.uniform(keys[0], (1, IN), jnp.float32) - 0.5) * 3.0 ** (columns / IN - 0.5)
    noise = jnp.clip(jax.random.normal(keys[1], (OUT, IN), jnp.float32), -4.0, 4.0)
    return (noise * col_scale).astype(jnp.bfloat16)


def shard_levels(key, shape, pieces, smallest, top_value):
    level, own = 1.0, jax.random.fold_in(key, 6)
    for position, parts in pieces:
        draws = jnp.exp(jax.random.uniform(jax.random.fold_in(own, position), (parts,), jnp.float32, smallest / len(pieces), top_value / len(pieces)))
        level = level * jnp.repeat(draws, shape[position] // parts).reshape([-1 if axis == position else 1 for axis in range(len(shape))])
    return level


def setup_inputs(seed: int = 0) -> dict:
    seeds = jax.random.split(jax.random.key(seed), 4)
    return {
        "activations": draw_activations(jax.random.fold_in(seeds[3], 71), 0),
        "weight": draw_weight(jax.random.fold_in(seeds[3], 71), 0),
        "thresholds": jnp.clip(0.5 + 1.0 * jax.random.uniform(seeds[2], (OUT,), jnp.float32) ** shard_levels(seeds[2], (OUT,), ((0, 16),), -0.2, 0.2), 0.5, 1.5),
    }


gate_slope = 2.0
small_eps = 1e-06

def reference(activations, weight, thresholds):
    blocks = activations.reshape(N_DP, TOKENS // N_DP, IN)

    def accumulate(total, block):
        return (total + lax.optimization_barrier(jnp.sum(jnp.square(block.astype(jnp.float32)), axis=0)), None)
    squares, _ = lax.scan(accumulate, jnp.zeros((IN,), jnp.float32), blocks)
    col_norm = jnp.sqrt(squares)
    rows = weight.reshape(N_DP, OUT // N_DP, IN)
    limits = thresholds.reshape(N_DP, OUT // N_DP)

    def prune(pair):
        block, limit = pair
        wide = block.astype(jnp.float32)
        scores = jnp.abs(wide) * col_norm[None, :]
        row_mean = lax.optimization_barrier(jnp.sum(scores, axis=1, keepdims=True)) / IN + small_eps
        kept_share = jnp.clip((scores / row_mean - limit[:, None]) * gate_slope + 0.5, 0.0, 1.0)
        return (wide * kept_share).astype(jnp.bfloat16)
    return lax.map(prune, (rows, limits)).reshape(OUT, IN)
```

```python
import functools

import jax
import jax.numpy as jnp
import numpy as np
from jax import lax
from jax.experimental import pallas as pl
from jax.experimental.pallas import tpu as pltpu
from jax.sharding import PartitionSpec as P


gate_slope = 2.0
small_eps = 1e-06


def exchange_plan(n):
    if n != 16:
        if n & (n - 1) == 0:
            return [[i ^ s for i in range(n)] for s in list(range(n // 2, n)) + list(range(n // 2))]
        return [[(i + s) % n for i in range(n)] for s in range(n)]
    plan = []
    for o, q in zip((0, 1, 2, 3), (1, 2, 3, 0)):
        plan.append([(12 - 4 * (i // 4)) + (i % 4 ^ o) if i // 4 in (1, 2) else i ^ q for i in range(n)])
    for hop in ((1, 3, 0, 2), (2, 0, 3, 1)):
        for o in (0, 1, 2, 3):
            plan.append([4 * hop[i // 4] + (i % 4 ^ o) for i in range(n)])
    for o, q in zip((0, 1, 2, 3), (1, 2, 3, 0)):
        plan.append([(12 - 4 * (i // 4)) + (i % 4 ^ o) if i // 4 in (0, 3) else i ^ q for i in range(n)])
    return plan


def take_block(table, weight, step, rows):
    cols = weight.shape[1]
    tile = rows // 4 if rows % 64 == 0 else rows

    def body(_, src, dst):
        dst[...] = src[...]

    return pl.pallas_call(
        body,
        grid_spec=pltpu.PrefetchScalarGridSpec(
            num_scalar_prefetch=1,
            grid=(rows // tile,),
            in_specs=[pl.BlockSpec((tile, cols), lambda r, t: (t[step] * (rows // tile) + r, 0))],
            out_specs=pl.BlockSpec((tile, cols), lambda r, t: (r, 0)),
        ),
        out_shape=jax.ShapeDtypeStruct((rows, cols), weight.dtype),
        cost_estimate=pl.CostEstimate(flops=0, bytes_accessed=4 * rows * cols, transcendentals=0),
    )(table, weight)


def prune_block(table, block, norm, slope, shift, step, n, out):
    rows, cols = block.shape
    tile = rows // 4 if rows % 64 == 0 else rows

    def body(_, block_ref, norm_ref, slope_ref, shift_ref, *rest):
        wide = block_ref[...].astype(jnp.float32)
        scores = jnp.abs(wide) * norm_ref[...]
        share = jnp.clip(scores * slope_ref[...] + shift_ref[...], 0.0, 1.0)
        rest[-1][...] = (wide * share).astype(jnp.bfloat16)

    in_specs = [
        pl.BlockSpec((tile, cols), lambda r, t: (r, 0)),
        pl.BlockSpec((1, cols), lambda r, t: (0, 0)),
        pl.BlockSpec((tile, 1), lambda r, t: (r, 0)),
        pl.BlockSpec((tile, 1), lambda r, t: (r, 0)),
    ]
    operands = [table, block, norm, slope, shift]
    aliases = {}
    if out is not None:
        in_specs.append(pl.BlockSpec(memory_space=pl.ANY))
        operands.append(out)
        aliases = {5: 0}
    return pl.pallas_call(
        body,
        grid_spec=pltpu.PrefetchScalarGridSpec(
            num_scalar_prefetch=1,
            grid=(rows // tile,),
            in_specs=in_specs,
            out_specs=pl.BlockSpec((tile, cols), lambda r, t: (r, t[step])),
        ),
        out_shape=jax.ShapeDtypeStruct((rows, n * cols), jnp.bfloat16),
        input_output_aliases=aliases,
        cost_estimate=pl.CostEstimate(flops=6 * rows * cols, bytes_accessed=4 * rows * cols, transcendentals=0),
    )(*operands)


def per_device(n, n_mp, activations, weight, thresholds):
    plan = exchange_plan(n)
    targets = np.array(plan, np.int32).T
    sources = np.stack([np.argsort(p) for p in plan]).astype(np.int32).T
    me = lax.axis_index("dp")
    to = lax.dynamic_index_in_dim(jnp.asarray(targets), me, 0, keepdims=False)
    come = lax.dynamic_index_in_dim(jnp.asarray(sources), me, 0, keepdims=False)
    cols = weight.shape[1]
    rows = weight.shape[0] // n
    total_cols = cols * n * n_mp

    def send(x, step):
        return lax.ppermute(x, "dp", [(i, plan[step][i]) for i in range(n)])

    blocks = []
    for k in range(n):
        blocks.append(take_block(to, weight, k, rows))
    arrived = [send(blocks[k], k) for k in range(n)]

    partial_value = jnp.sum(jnp.square(activations.astype(jnp.float32)), axis=0)
    parts = jnp.take(partial_value.reshape(n, cols), to, axis=0)
    got = [send(parts[k], k) for k in range(n)]
    col_norm = jnp.sqrt(functools.reduce(jnp.add, got))
    row_part = jnp.sum(jnp.abs(weight.astype(jnp.float32)) * col_norm[None, :], axis=1).reshape(n, rows)
    notes = jnp.concatenate([jnp.take(row_part, to, axis=0), jnp.broadcast_to(col_norm, (n, cols))], axis=1)
    noted = [send(notes[k], k) for k in range(n)]
    row_total = lax.psum(functools.reduce(jnp.add, [v[:rows] for v in noted]), "mp")
    row_mean = row_total / total_cols + small_eps
    slope = (gate_slope / row_mean)[:, None]
    shift = (0.5 - gate_slope * thresholds)[:, None]

    if cols % 128 == 0:
        out = None
        late = list(range(n // 2 - 2, n // 2))
        for k in [v for v in range(n) if v not in late] + late:
            out = prune_block(come, arrived[k], noted[k][rows:][None, :], slope, shift, k, n, out)
        return out
    out = jnp.zeros((rows, n * cols), jnp.bfloat16)
    for k in range(n):
        wide = arrived[k].astype(jnp.float32)
        share = jnp.clip(jnp.abs(wide) * noted[k][None, rows:] * slope + shift, 0.0, 1.0)
        out = lax.dynamic_update_slice(out, (wide * share).astype(jnp.bfloat16), (0, come[k] * cols))
    return out


def solution(mesh):
    placed = (P("dp", "mp"), P(None, ("mp", "dp")), P("dp"))
    return jax.shard_map(
        functools.partial(per_device, mesh.shape["dp"], mesh.shape["mp"]),
        mesh=mesh,
        in_specs=placed,
        out_specs=P("dp", "mp"),
        check_vma=False,
    )
```

```python
import functools

import jax
import jax.numpy as jnp
import numpy as np
from jax import lax
from jax.experimental import pallas as pl
from jax.experimental.pallas import tpu as pltpu
from jax.sharding import PartitionSpec as P


gate_slope = 2.0
small_eps = 1e-06


def target(step, i, n, where=np.where):
    if n != 16:
        if n & (n - 1):
            return (i + step) % n
        return i ^ (step + n // 2) % n
    group, o = step // 4, step % 4
    place, seat = i // 4, i % 4
    if group in (0, 3):
        inner = (place == 1) | (place == 2)
        return where(inner == (group == 0), 12 - 4 * place + (seat ^ o), i ^ (o + 1) % 4)
    hop = (2 * place + 1) % 5 if group == 1 else (3 * place + 2) % 5
    return 4 * hop + (seat ^ o)


def prune_block(come, block, note, slope, shift, step, n, out, near):
    rows, cols = block.shape
    parts = 4 if rows % 64 == 0 else 1
    tile = rows // parts

    def body(come_ref, block_ref, note_ref, slope_ref, shift_ref, *rest):
        out_ref, wide_ref, done_ref, in_sem, out_sem = rest[-5:]
        at = pl.multiple_of(come_ref[step] * cols, 128)
        pieces = [pl.ds(p * tile, tile) for p in range(parts)]
        gets = []
        if not near:
            gets = [pltpu.make_async_copy(block_ref.at[s], wide_ref.at[s], in_sem.at[p]) for p, s in enumerate(pieces)]
        puts = [
            pltpu.make_async_copy(done_ref.at[s], out_ref.at[s, pl.ds(at, cols)], out_sem.at[p])
            for p, s in enumerate(pieces)
        ]
        for get in gets:
            get.start()
        norm = note_ref[:, rows:]
        for p, s in enumerate(pieces):
            if not near:
                gets[p].wait()
            wide = (block_ref if near else wide_ref)[s].astype(jnp.float32)
            share = jnp.clip(jnp.abs(wide) * norm * slope_ref[s] + shift_ref[s], 0.0, 1.0)
            done_ref[s] = (wide * share).astype(jnp.bfloat16)
            puts[p].start()
        for put in puts:
            put.wait()

    here, there = pl.BlockSpec(memory_space=pltpu.VMEM), pl.BlockSpec(memory_space=pl.ANY)
    in_specs = [pl.BlockSpec(memory_space=pltpu.SMEM), here if near else there, here, here, here]
    operands = [come, block, note, slope, shift]
    if out is not None:
        in_specs.append(there)
        operands.append(out)
    return pl.pallas_call(
        body,
        in_specs=in_specs,
        out_specs=there,
        scratch_shapes=[pltpu.VMEM((rows, cols), jnp.bfloat16)] * 2 + [pltpu.SemaphoreType.DMA((parts,))] * 2,
        out_shape=jax.ShapeDtypeStruct((rows, n * cols), jnp.bfloat16),
        input_output_aliases={} if out is None else {5: 0},
        cost_estimate=pl.CostEstimate(flops=6 * rows * cols, bytes_accessed=4 * rows * cols, transcendentals=0),
    )(*operands)


def per_device(n, n_mp, activations, weight, thresholds):
    ids = np.arange(n)
    plan = [target(k, ids, n) for k in range(n)]
    me = lax.axis_index("dp")
    tables = np.stack([np.stack(plan, 1), np.stack([np.argsort(p) for p in plan], 1)]).astype(np.int32)
    cols = weight.shape[1]
    rows = weight.shape[0] // n
    total_cols = cols * n * n_mp

    def send(x, step):
        return lax.ppermute(x, "dp", [(i, int(plan[step][i])) for i in range(n)])

    def take(source, step):
        return lax.dynamic_slice(source, (target(step, me, n, jnp.where) * rows, 0), (rows, cols))

    first = take(weight, 0)
    rest, _ = lax.optimization_barrier((weight, first))
    blocks = [first] + [take(rest, k) for k in range(1, n)]
    arrived = [send(blocks[k], k) for k in range(n)]

    to = lax.dynamic_index_in_dim(jnp.asarray(tables[0]), me, 0, keepdims=False)
    come = lax.dynamic_index_in_dim(jnp.asarray(tables[1]), me, 0, keepdims=False)
    partial_value = jnp.sum(jnp.square(activations.astype(jnp.float32)), axis=0)
    parts = jnp.take(partial_value.reshape(n, cols), to, axis=0)
    got = [send(parts[k], k) for k in range(n)]
    col_norm = jnp.sqrt(functools.reduce(jnp.add, got))
    row_part = jnp.sum(jnp.abs(weight.astype(jnp.float32)) * col_norm[None, :], axis=1).reshape(n, rows)
    notes = jnp.concatenate([jnp.take(row_part, to, axis=0), jnp.broadcast_to(col_norm, (n, cols))], axis=1)
    noted = [send(notes[k : k + 1], k) for k in range(n)]
    row_total = lax.psum(functools.reduce(jnp.add, [v[0, :rows] for v in noted]), "mp")
    row_mean = row_total / total_cols + small_eps
    slope = (gate_slope / row_mean)[:, None]
    shift = (0.5 - gate_slope * thresholds)[:, None]

    late = list(range(n // 2 - 2, n // 2))
    order = [v for v in range(n) if v not in late] + late
    if cols % 128 == 0 and rows % 128 == 0:
        out = None
        for k in order:
            near = k in order[-2:]
            out = prune_block(come, arrived[k], noted[k], slope, shift, k, n, out, near)
        return out
    out = jnp.zeros((rows, n * cols), jnp.bfloat16)
    for k in order:
        wide = arrived[k].astype(jnp.float32)
        share = jnp.clip(jnp.abs(wide) * noted[k][:, rows:] * slope + shift, 0.0, 1.0)
        out = lax.dynamic_update_slice(out, (wide * share).astype(jnp.bfloat16), (0, come[k] * cols))
    return out


def solution(mesh):
    placed = (P("dp", "mp"), P(None, ("mp", "dp")), P("dp"))
    n = mesh.shape["dp"]
    return jax.shard_map(
        functools.partial(per_device, n, mesh.shape["mp"]),
        mesh=mesh,
        in_specs=placed,
        out_specs=P("dp", "mp"),
        check_vma=False,
    )
```

```python
import functools

import jax
import jax.numpy as jnp
import numpy as np
from jax import lax
from jax.experimental import pallas as pl
from jax.experimental.pallas import tpu as pltpu
from jax.sharding import PartitionSpec as P


gate_slope = 2.0
small_eps = 1e-06


def target(step, i, n, where=np.where):
    if n != 16:
        if n & (n - 1):
            return (i + step) % n
        return i ^ (step + n // 2) % n
    group, o = step // 4, step % 4
    place, seat = i >> 2, i & 3
    if group in (1, 3):
        inner = (place == 1) | (place == 2)
        return where(inner == (group == 1), 12 - 4 * place + (seat ^ o), i ^ ((o + 1) % 4))
    hop = ((place & 1) << 1) + ((place >> 1) ^ 1) if group == 0 else (((place & 1) ^ 1) << 1) + (place >> 1)
    return 4 * hop + (seat ^ o)


def pieces_of(n, rows):
    cut = rows // 4
    pieces = []
    for step in range(n):
        if rows % 64 or step not in (0, n // 2 - 1):
            pieces.append((step, 0, rows))
        else:
            split = cut if step == 0 else rows - cut
            pieces += [(step, 0, split), (step, split, rows - split)]
    return pieces


def prune_block(come, block, note, slope, shift, step, top, n, out, near):
    rows, cols = slope.shape[0], block.shape[1]
    size = block.shape[0]
    parts = max(size // 128, 1)
    tile = size // parts

    def body(come_ref, block_ref, note_ref, slope_ref, shift_ref, *rest):
        out_ref, wide_ref, done_ref, in_sem, out_sem = rest[-5:]
        at = pl.multiple_of(come_ref[step] * cols, 128)
        here = [pl.ds(p * tile, tile) for p in range(parts)]
        there = [pl.ds(top + p * tile, tile) for p in range(parts)]
        gets = []
        if not near:
            gets = [pltpu.make_async_copy(block_ref.at[s], wide_ref.at[s], in_sem.at[p]) for p, s in enumerate(here)]
        for get in gets:
            get.start()
        norm = note_ref[:, rows:]
        puts = []
        for p, (s, d) in enumerate(zip(here, there)):
            if not near:
                gets[p].wait()
            wide = (block_ref if near else wide_ref)[s].astype(jnp.float32)
            share = jnp.clip(jnp.abs(wide) * norm * slope_ref[d] + shift_ref[d], 0.0, 1.0)
            done_ref[s] = (wide * share).astype(jnp.bfloat16)
            puts.append(pltpu.make_async_copy(done_ref.at[s], out_ref.at[d, pl.ds(at, cols)], out_sem.at[p]))
            puts[-1].start()
        for put in puts:
            put.wait()

    here, there = pl.BlockSpec(memory_space=pltpu.VMEM), pl.BlockSpec(memory_space=pl.ANY)
    in_specs = [pl.BlockSpec(memory_space=pltpu.SMEM), here if near else there, here, here, here]
    operands = [come, block, note, slope, shift]
    if out is not None:
        in_specs.append(there)
        operands.append(out)
    return pl.pallas_call(
        body,
        in_specs=in_specs,
        out_specs=there,
        scratch_shapes=[pltpu.VMEM((size, cols), jnp.bfloat16)] * 2 + [pltpu.SemaphoreType.DMA((parts,))] * 2,
        out_shape=jax.ShapeDtypeStruct((rows, n * cols), jnp.bfloat16),
        input_output_aliases={} if out is None else {5: 0},
        cost_estimate=pl.CostEstimate(flops=6 * size * cols, bytes_accessed=4 * size * cols, transcendentals=0),
    )(*operands)


def per_device(n, n_mp, activations, weight, thresholds):
    ids = np.arange(n)
    plan = [target(k, ids, n) for k in range(n)]
    me = lax.axis_index("dp")
    tables = np.stack([np.stack(plan, 1), np.stack([np.argsort(p) for p in plan], 1)]).astype(np.int32)
    cols = weight.shape[1]
    rows = weight.shape[0] // n
    total_cols = cols * n * n_mp

    pieces = pieces_of(n, rows)

    def send(x, step):
        return lax.ppermute(x, "dp", [(i, int(plan[step][i])) for i in range(n)])

    def take(source, step, top, size):
        return lax.dynamic_slice(source, (target(step, me, n, jnp.where) * rows + top, 0), (size, cols))

    blocks, source = [], weight
    for piece in pieces:
        blocks.append(take(source, *piece))
        if len(blocks) <= 2:
            source, _ = lax.optimization_barrier((source, blocks[-1]))
    arrived = [send(block, step) for block, (step, _, _) in zip(blocks, pieces)]

    to = lax.dynamic_index_in_dim(jnp.asarray(tables[0]), me, 0, keepdims=False)
    come = lax.dynamic_index_in_dim(jnp.asarray(tables[1]), me, 0, keepdims=False)
    partial_value = jnp.sum(jnp.square(activations.astype(jnp.float32)), axis=0)
    parts = jnp.take(partial_value.reshape(n, cols), to, axis=0)
    got = [send(parts[k], k) for k in range(n)]
    col_norm = jnp.sqrt(functools.reduce(jnp.add, got))
    row_part = jnp.sum(jnp.abs(weight.astype(jnp.float32)) * col_norm[None, :], axis=1).reshape(n, rows)
    notes = jnp.concatenate([jnp.take(row_part, to, axis=0), jnp.broadcast_to(col_norm, (n, cols))], axis=1)
    noted = [send(notes[k : k + 1], k) for k in range(n)]
    row_total = lax.psum(functools.reduce(jnp.add, [v[0, :rows] for v in noted]), "mp")
    row_mean = row_total / total_cols + small_eps
    slope = (gate_slope / row_mean)[:, None]
    shift = (0.5 - gate_slope * thresholds)[:, None]

    late = [i for i, (step, _, _) in enumerate(pieces) if step in (n // 2 - 2, n // 2 - 1)]
    order = [i for i in range(len(pieces)) if i not in late] + late
    if cols % 128 == 0 and rows % 128 == 0:
        out = None
        for i in order:
            step, top, _ = pieces[i]
            near = i in order[-2:]
            out = prune_block(come, arrived[i], noted[step], slope, shift, step, top, n, out, near)
        return out
    out = jnp.zeros((rows, n * cols), jnp.bfloat16)
    for i in order:
        step, top, size = pieces[i]
        wide = arrived[i].astype(jnp.float32)
        ours = slice(top, top + size)
        share = jnp.clip(jnp.abs(wide) * noted[step][:, rows:] * slope[ours] + shift[ours], 0.0, 1.0)
        out = lax.dynamic_update_slice(out, (wide * share).astype(jnp.bfloat16), (top, come[step] * cols))
    return out


def solution(mesh):
    placed = (P("dp", "mp"), P(None, ("mp", "dp")), P("dp"))
    n, n_mp = mesh.shape["dp"], mesh.shape["mp"]
    return jax.shard_map(
        functools.partial(per_device, n, n_mp),
        mesh=mesh,
        in_specs=placed,
        out_specs=P("dp", "mp"),
        check_vma=False,
    )
```

```python
import functools

import jax
import jax.numpy as jnp
import numpy as np
from jax import lax
from jax.experimental import pallas as pl
from jax.experimental.pallas import tpu as pltpu
from jax.sharding import PartitionSpec as P


gate_slope = 2.0
small_eps = 1e-06


pairs = (0, 3, 6, 7)


def target(step, i, n, where=np.where):
    if n != 16:
        if n & (n - 1):
            return (i + step) % n
        return i ^ (step + n // 2) % n
    kind = "pair" if step % 8 in pairs else "ring"
    o = sum((k in pairs) == (kind == "pair") for k in range(step % 8))
    place, seat = i >> 2, i & 3
    if kind == "pair":
        inner = (place == 1) | (place == 2)
        return where(inner == (step < 8), 12 - 4 * place + (seat ^ o), i ^ (1, 0, 2, 3)[o])
    hop = ((place & 1) << 1) + ((place >> 1) ^ 1) if step < 8 else (((place & 1) ^ 1) << 1) + (place >> 1)
    return 4 * hop + (seat ^ o)


def source(step, i, n, where=np.where):
    if n != 16:
        return (i - step) % n if n & (n - 1) else target(step, i, n)
    return target(step, i, n, where) if step % 8 in pairs else target((step + 8) % 16, i, n)


def pieces_of(n, rows):
    pieces = []
    for step in range(n):
        if rows % 64 or step != n // 2 - 1:
            pieces.append((step, 0, rows))
        else:
            split = rows - rows // 4
            pieces += [(step, 0, split), (step, split, rows - split)]
    return pieces


near_squares, near_notes = 4, 4


def gather_sums(parts, n, near, extra=None):
    near = near if n % near == 0 else 1
    far = n // near
    inside = [[group * near + member for member in range(near)] for group in range(far)]
    across = [[group * near + member for group in range(far)] for member in range(near)]
    width = parts.shape[1]
    parts = parts.reshape(far, near, width).swapaxes(0, 1)
    if near > 1:
        parts = lax.all_to_all(parts, "dp", 0, 0, axis_index_groups=inside, tiled=True)
    parts = jnp.sum(parts, axis=0)
    if extra is not None:
        parts = jnp.concatenate([parts, jnp.broadcast_to(extra, (far, extra.shape[0]))], axis=1)
    parts = lax.all_to_all(parts, "dp", 0, 0, axis_index_groups=across, tiled=True)
    total = jnp.sum(parts[:, :width], axis=0)
    if extra is None:
        return total
    extras = jnp.broadcast_to(parts[:, width:], (near, far, extra.shape[0]))
    if near > 1:
        extras = lax.all_to_all(extras, "dp", 0, 0, axis_index_groups=inside, tiled=True)
    return total, extras.reshape(n, extra.shape[0])


def prune_block(block, norms, slope, shift, step, top, n, out, near):
    rows, cols = slope.shape[0], block.shape[1]
    size = block.shape[0]
    tile, lines = 128, 128 if near else 32
    parts = size // tile

    def body(block_ref, norms_ref, slope_ref, shift_ref, *rest):
        out_ref, wide_ref, done_ref, in_sem, out_sem = rest[-5:]
        owner = source(step, lax.axis_index("dp"), n, jnp.where)
        at = pl.multiple_of(owner * cols, 128)

        def get(p):
            part = pl.ds(p * tile, tile)
            return pltpu.make_async_copy(block_ref.at[part], wide_ref.at[part], in_sem.at[p])

        def put(p):
            there = out_ref.at[pl.ds(top + p * tile, tile), pl.ds(at, cols)]
            return pltpu.make_async_copy(done_ref.at[pl.ds(p * tile, tile)], there, out_sem.at[p])

        if not near:
            for p in range(parts):
                get(p).start()
        norm = norms_ref[...][step : step + 1, :]
        block_rows = block_ref if near else wide_ref

        @pl.loop(0, parts)
        def _(p):
            if not near:
                get(p).wait()

            @pl.loop(0, tile // lines)
            def _(q):
                first = pl.multiple_of(p * tile + q * lines, lines)
                here, ours = pl.ds(first, lines), pl.ds(top + first, lines)
                wide = block_rows[here].astype(jnp.float32)
                share = jnp.clip(jnp.abs(wide) * norm * slope_ref[ours] + shift_ref[ours], 0.0, 1.0)
                done_ref[here] = (wide * share).astype(jnp.bfloat16)

            put(p).start()

        @pl.loop(0, parts)
        def _(p):
            put(p).wait()

    here, there = pl.BlockSpec(memory_space=pltpu.VMEM), pl.BlockSpec(memory_space=pl.ANY)
    in_specs = [here if near else there, here, here, here]
    if near:
        block = pltpu.with_memory_space_constraint(block, pltpu.VMEM)
    operands = [block, norms, slope, shift]
    if out is not None:
        in_specs.append(there)
        operands.append(out)
    return pl.pallas_call(
        body,
        in_specs=in_specs,
        out_specs=there,
        scratch_shapes=[pltpu.VMEM((size, cols), jnp.bfloat16)] * 2 + [pltpu.SemaphoreType.DMA((parts,))] * 2,
        out_shape=jax.ShapeDtypeStruct((rows, n * cols), jnp.bfloat16),
        input_output_aliases={} if out is None else {4: 0},
        cost_estimate=pl.CostEstimate(flops=6 * size * cols, bytes_accessed=4 * size * cols, transcendentals=0),
    )(*operands)


def per_device(n, n_mp, activations, weight, thresholds):
    ids = np.arange(n)
    plan = [target(k, ids, n) for k in range(n)]
    me = lax.axis_index("dp")
    cols = weight.shape[1]
    rows = weight.shape[0] // n
    total_cols = cols * n * n_mp

    pieces = pieces_of(n, rows)

    def send(x, step):
        return lax.ppermute(x, "dp", [(i, int(plan[step][i])) for i in range(n)])

    def take(rest, step, top, size):
        return lax.dynamic_slice(rest, (target(step, me, n, jnp.where) * rows + top, 0), (size, cols))

    first = take(weight, *pieces[0])
    rest, _ = lax.optimization_barrier((weight, first))
    blocks = [first] + [take(rest, *piece) for piece in pieces[1:]]
    arrived = [send(block, step) for block, (step, _, _) in zip(blocks, pieces)]

    partial_value = jnp.sum(jnp.square(activations.astype(jnp.float32)), axis=0)
    squares = gather_sums(partial_value.reshape(n, cols), n, near_squares)
    col_norm = jnp.sqrt(squares)
    row_part = jnp.sum(jnp.abs(weight.astype(jnp.float32)) * col_norm[None, :], axis=1).reshape(n, rows)
    row_part, norms = gather_sums(row_part, n, near_notes, col_norm)
    by_step = np.stack([source(k, ids, n) for k in range(n)], 1)
    by_step = by_step % near_notes * (n // near_notes) + by_step // near_notes
    by_step = lax.dynamic_index_in_dim(jnp.asarray(by_step.astype(np.int32)), me, 0, keepdims=False)
    norms = jnp.take(norms, by_step, axis=0, mode="clip")
    row_total = lax.psum(row_part, "mp")
    row_mean = row_total / total_cols + small_eps
    slope = (gate_slope / row_mean)[:, None]
    shift = (0.5 - gate_slope * thresholds)[:, None]

    late = [i for i, (step, _, _) in enumerate(pieces) if 5 * n // 16 <= step < n // 2]
    order = [i for i in range(len(pieces)) if i not in late] + late
    if cols % 128 == 0 and rows % 128 == 0:
        norms, slope, shift = [pltpu.with_memory_space_constraint(v, pltpu.VMEM) for v in (norms, slope, shift)]
        out = None
        for i in order:
            step, top, _ = pieces[i]
            near = i in order[-2:]
            out = prune_block(arrived[i], norms, slope, shift, step, top, n, out, near)
        return out
    out = jnp.zeros((rows, n * cols), jnp.bfloat16)
    for i in order:
        step, top, size = pieces[i]
        wide = arrived[i].astype(jnp.float32)
        ours = slice(top, top + size)
        owner = source(step, me, n, jnp.where)
        share = jnp.clip(jnp.abs(wide) * norms[step] * slope[ours] + shift[ours], 0.0, 1.0)
        out = lax.dynamic_update_slice(out, (wide * share).astype(jnp.bfloat16), (top, owner * cols))
    return out


def solution(mesh):
    placed = (P("dp", "mp"), P(None, ("mp", "dp")), P("dp"))
    n, n_mp = mesh.shape["dp"], mesh.shape["mp"]
    return jax.shard_map(
        functools.partial(per_device, n, n_mp),
        mesh=mesh,
        in_specs=placed,
        out_specs=P("dp", "mp"),
        check_vma=False,
    )
```

```python
import functools

import jax
import jax.numpy as jnp
import numpy as np
from jax import lax
from jax.experimental import pallas as pl
from jax.experimental.pallas import tpu as pltpu
from jax.sharding import PartitionSpec as P


gate_slope = 2.0
small_eps = 1e-06


pairs = (0, 3, 6, 7)


def target(step, i, n, where=np.where):
    if n != 16:
        if n & (n - 1):
            return (i + step) % n
        return i ^ (step + n // 2) % n
    kind = "pair" if step % 8 in pairs else "ring"
    o = sum((k in pairs) == (kind == "pair") for k in range(step % 8))
    place, seat = i >> 2, i & 3
    if kind == "pair":
        inner = (place == 1) | (place == 2)
        return where(inner == (step < 8), 12 - 4 * place + (seat ^ o), i ^ (1, 0, 2, 3)[o])
    hop = ((place & 1) << 1) + ((place >> 1) ^ 1) if step < 8 else (((place & 1) ^ 1) << 1) + (place >> 1)
    return 4 * hop + (seat ^ o)


def source(step, i, n, where=np.where):
    if n != 16:
        return (i - step) % n if n & (n - 1) else target(step, i, n)
    return target(step, i, n, where) if step % 8 in pairs else target((step + 8) % 16, i, n)


def pieces_of(n, rows):
    pieces = []
    for step in range(n):
        if rows % 64 or step != n // 2 - 1:
            pieces.append((step, 0, rows))
        else:
            split = rows - rows // 4
            pieces += [(step, 0, split), (step, split, rows - split)]
    return pieces


def group_size(n):
    return 4 if n % 4 == 0 else 1


def gather_sums(parts, n, extra=None):
    near = group_size(n)
    far = n // near
    inside = [[group * near + member for member in range(near)] for group in range(far)]
    across = [[group * near + member for group in range(far)] for member in range(near)]
    width = parts.shape[1]
    parts = parts.reshape(far, near, width).swapaxes(0, 1)
    if near > 1:
        parts = lax.all_to_all(parts, "dp", 0, 0, axis_index_groups=inside, tiled=True)
    parts = jnp.sum(parts, axis=0)
    if extra is not None:
        parts = jnp.concatenate([parts, jnp.broadcast_to(extra, (far, extra.shape[0]))], axis=1)
    parts = lax.all_to_all(parts, "dp", 0, 0, axis_index_groups=across, tiled=True)
    total = jnp.sum(parts[:, :width], axis=0)
    if extra is None:
        return total
    extras = jnp.broadcast_to(parts[:, width:], (near, far, extra.shape[0]))
    if near > 1:
        extras = lax.all_to_all(extras, "dp", 0, 0, axis_index_groups=inside, tiled=True)
    return total, extras.reshape(n, extra.shape[0])


def prune_block(block, norms, slope, shift, step, top, n, out, near):
    rows, cols = slope.shape[0], block.shape[1]
    size = block.shape[0]
    tile, lines = 128, 128 if near else 32
    parts = size // tile

    def body(block_ref, norms_ref, slope_ref, shift_ref, *rest):
        out_ref, wide_ref, done_ref, in_sem, out_sem = rest[-5:]
        owner = source(step, lax.axis_index("dp"), n, jnp.where)
        at = pl.multiple_of(owner * cols, 128)

        def get(p):
            part = pl.ds(p * tile, tile)
            return pltpu.make_async_copy(block_ref.at[part], wide_ref.at[part], in_sem.at[p])

        def put(p):
            there = out_ref.at[pl.ds(top + p * tile, tile), pl.ds(at, cols)]
            return pltpu.make_async_copy(done_ref.at[pl.ds(p * tile, tile)], there, out_sem.at[p])

        if not near:
            for p in range(parts):
                get(p).start()
        norm = norms_ref[...][step : step + 1, :]
        block_rows = block_ref if near else wide_ref

        @pl.loop(0, parts)
        def _(p):
            if not near:
                get(p).wait()

            @pl.loop(0, tile // lines)
            def _(q):
                first = pl.multiple_of(p * tile + q * lines, lines)
                here, ours = pl.ds(first, lines), pl.ds(top + first, lines)
                wide = block_rows[here].astype(jnp.float32)
                share = jnp.clip(jnp.abs(wide) * norm * slope_ref[ours] + shift_ref[ours], 0.0, 1.0)
                done_ref[here] = (wide * share).astype(jnp.bfloat16)

            put(p).start()

        @pl.loop(0, parts)
        def _(p):
            put(p).wait()

    here, there = pl.BlockSpec(memory_space=pltpu.VMEM), pl.BlockSpec(memory_space=pl.ANY)
    in_specs = [here if near else there, here, here, here]
    if near:
        block = pltpu.with_memory_space_constraint(block, pltpu.VMEM)
    operands = [block, norms, slope, shift]
    if out is not None:
        in_specs.append(there)
        operands.append(out)
    return pl.pallas_call(
        body,
        in_specs=in_specs,
        out_specs=there,
        scratch_shapes=[pltpu.VMEM((size, cols), jnp.bfloat16)] * 2 + [pltpu.SemaphoreType.DMA((parts,))] * 2,
        out_shape=jax.ShapeDtypeStruct((rows, n * cols), jnp.bfloat16),
        input_output_aliases={} if out is None else {4: 0},
        cost_estimate=pl.CostEstimate(flops=6 * size * cols, bytes_accessed=4 * size * cols, transcendentals=0),
    )(*operands)


def per_device(n, n_mp, activations, weight, thresholds):
    ids = np.arange(n)
    plan = [target(k, ids, n) for k in range(n)]
    me = lax.axis_index("dp")
    cols = weight.shape[1]
    rows = weight.shape[0] // n
    total_cols = cols * n * n_mp

    pieces = pieces_of(n, rows)

    def send(x, step):
        return lax.ppermute(x, "dp", [(i, int(plan[step][i])) for i in range(n)])

    def take(rest, step, top, size):
        return lax.dynamic_slice(rest, (target(step, me, n, jnp.where) * rows + top, 0), (size, cols))

    first = take(weight, *pieces[0])
    rest, _ = lax.optimization_barrier((weight, first))
    blocks = [first] + [take(rest, *piece) for piece in pieces[1:]]
    arrived = [send(block, step) for block, (step, _, _) in zip(blocks, pieces)]

    partial_value = jnp.sum(jnp.square(activations.astype(jnp.float32)), axis=0)
    squares = gather_sums(partial_value.reshape(n, cols), n)
    col_norm = jnp.sqrt(squares)
    row_part = jnp.sum(jnp.abs(weight.astype(jnp.float32)) * col_norm[None, :], axis=1).reshape(n, rows)
    row_part, norms = gather_sums(row_part, n, col_norm)
    by_step = np.stack([source(k, ids, n) for k in range(n)], 1)
    by_step = by_step % group_size(n) * (n // group_size(n)) + by_step // group_size(n)
    by_step = lax.dynamic_index_in_dim(jnp.asarray(by_step.astype(np.int32)), me, 0, keepdims=False)
    norms = jnp.take(norms, by_step, axis=0, mode="clip")
    row_total = lax.psum(row_part, "mp")
    row_mean = row_total / total_cols + small_eps
    slope = (gate_slope / row_mean)[:, None]
    shift = (0.5 - gate_slope * thresholds)[:, None]

    late = [i for i, (step, _, _) in enumerate(pieces) if 5 * n // 16 <= step < n // 2]
    order = [i for i in range(len(pieces)) if i not in late] + late
    if cols % 128 == 0 and rows % 128 == 0:
        norms, slope, shift = [pltpu.with_memory_space_constraint(v, pltpu.VMEM) for v in (norms, slope, shift)]
        out = None
        for i in order:
            step, top, _ = pieces[i]
            near = i in order[-2:]
            out = prune_block(arrived[i], norms, slope, shift, step, top, n, out, near)
        return out
    out = jnp.zeros((rows, n * cols), jnp.bfloat16)
    for i in order:
        step, top, size = pieces[i]
        wide = arrived[i].astype(jnp.float32)
        ours = slice(top, top + size)
        owner = source(step, me, n, jnp.where)
        share = jnp.clip(jnp.abs(wide) * norms[step] * slope[ours] + shift[ours], 0.0, 1.0)
        out = lax.dynamic_update_slice(out, (wide * share).astype(jnp.bfloat16), (top, owner * cols))
    return out


def solution(mesh):
    placed = (P("dp", "mp"), P(None, ("mp", "dp")), P("dp"))
    n, n_mp = mesh.shape["dp"], mesh.shape["mp"]
    return jax.shard_map(
        functools.partial(per_device, n, n_mp),
        mesh=mesh,
        in_specs=placed,
        out_specs=P("dp", "mp"),
        check_vma=False,
    )
```

```python
import functools

import jax
import jax.numpy as jnp
import numpy as np
from jax import lax
from jax.experimental import pallas as pl
from jax.experimental.pallas import tpu as pltpu
from jax.sharding import PartitionSpec as P


gate_slope = 2.0
small_eps = 1e-06


pairs = (0, 3, 6, 7)


def target(step, i, n, where=np.where):
    if n != 16:
        if n & (n - 1):
            return (i + step) % n
        return i ^ (step + n // 2) % n
    kind = "pair" if step % 8 in pairs else "ring"
    o = sum((k in pairs) == (kind == "pair") for k in range(step % 8))
    place, seat = i >> 2, i & 3
    if kind == "pair":
        inner = (place == 1) | (place == 2)
        return where(inner == (step < 8), 12 - 4 * place + (seat ^ o), i ^ (1, 0, 2, 3)[o])
    hop = ((place & 1) << 1) + ((place >> 1) ^ 1) if step < 8 else (((place & 1) ^ 1) << 1) + (place >> 1)
    return 4 * hop + (seat ^ o)


def source(step, i, n, where=np.where):
    if n != 16:
        return (i - step) % n if n & (n - 1) else target(step, i, n)
    return target(step, i, n, where) if step % 8 in pairs else target((step + 8) % 16, i, n)


def pieces_of(n, rows):
    pieces = []
    for step in range(n):
        if rows % 64 or step not in (0, n // 2 - 1):
            pieces.append((step, 0, rows))
        else:
            split = rows - rows // 4 if step else rows // 4
            pieces += [(step, 0, split), (step, split, rows - split)]
    return pieces


def group_size(n):
    return 4 if n % 4 == 0 else 1


def gather_sums(parts, n, extra=None):
    near = group_size(n)
    far = n // near
    inside = [[group * near + member for member in range(near)] for group in range(far)]
    across = [[group * near + member for group in range(far)] for member in range(near)]
    width = parts.shape[1]
    parts = parts.reshape(far, near, width).swapaxes(0, 1)
    if near > 1:
        parts = lax.all_to_all(parts, "dp", 0, 0, axis_index_groups=inside, tiled=True)
    parts = jnp.sum(parts, axis=0)
    if extra is not None:
        parts = jnp.concatenate([parts, jnp.broadcast_to(extra, (far, extra.shape[0]))], axis=1)
    parts = lax.all_to_all(parts, "dp", 0, 0, axis_index_groups=across, tiled=True)
    total = jnp.sum(parts[:, :width], axis=0)
    if extra is None:
        return total
    extras = jnp.broadcast_to(parts[:, width:], (near, far, extra.shape[0]))
    if near > 1:
        extras = lax.all_to_all(extras, "dp", 0, 0, axis_index_groups=inside, tiled=True)
    return total, extras.reshape(n, extra.shape[0])


def take_ahead(weight, step, top, size, n, rows):
    def body(weight_ref, out_ref, sem):
        start = pl.multiple_of(target(step, lax.axis_index("dp"), n, jnp.where) * rows + top, 128)
        copy = pltpu.make_async_copy(weight_ref.at[pl.ds(start, size)], out_ref, sem)
        copy.start()
        copy.wait()

    return pl.pallas_call(
        body,
        in_specs=[pl.BlockSpec(memory_space=pl.ANY)],
        out_specs=pl.BlockSpec(memory_space=pltpu.VMEM),
        scratch_shapes=[pltpu.SemaphoreType.DMA],
        out_shape=pltpu.VMEM((size, weight.shape[1]), weight.dtype),
    )(weight)


def prune_block(block, norms, slope, shift, step, top, n, out, near):
    rows, cols = slope.shape[0], block.shape[1]
    size = block.shape[0]
    tile, lines = 128, 128 if near else 32
    parts = size // tile

    def body(block_ref, norms_ref, slope_ref, shift_ref, *rest):
        out_ref, wide_ref, done_ref, in_sem, out_sem = rest[-5:]
        owner = source(step, lax.axis_index("dp"), n, jnp.where)
        at = pl.multiple_of(owner * cols, 128)

        def get(p):
            part = pl.ds(p * tile, tile)
            return pltpu.make_async_copy(block_ref.at[part], wide_ref.at[part], in_sem.at[p])

        def put(p):
            there = out_ref.at[pl.ds(top + p * tile, tile), pl.ds(at, cols)]
            return pltpu.make_async_copy(done_ref.at[pl.ds(p * tile, tile)], there, out_sem.at[p])

        if not near:
            for p in range(parts):
                get(p).start()
        norm = norms_ref[...][step : step + 1, :]
        block_rows = block_ref if near else wide_ref

        @pl.loop(0, parts)
        def _(p):
            if not near:
                get(p).wait()

            @pl.loop(0, tile // lines)
            def _(q):
                first = pl.multiple_of(p * tile + q * lines, lines)
                here, ours = pl.ds(first, lines), pl.ds(top + first, lines)
                wide = block_rows[here].astype(jnp.float32)
                share = jnp.clip(jnp.abs(wide) * norm * slope_ref[ours] + shift_ref[ours], 0.0, 1.0)
                done_ref[here] = (wide * share).astype(jnp.bfloat16)

            put(p).start()

        @pl.loop(0, parts)
        def _(p):
            put(p).wait()

    here, there = pl.BlockSpec(memory_space=pltpu.VMEM), pl.BlockSpec(memory_space=pl.ANY)
    in_specs = [here if near else there, here, here, here]
    if near:
        block = pltpu.with_memory_space_constraint(block, pltpu.VMEM)
    operands = [block, norms, slope, shift]
    if out is not None:
        in_specs.append(there)
        operands.append(out)
    return pl.pallas_call(
        body,
        in_specs=in_specs,
        out_specs=there,
        scratch_shapes=[pltpu.VMEM((size, cols), jnp.bfloat16)] * 2 + [pltpu.SemaphoreType.DMA((parts,))] * 2,
        out_shape=jax.ShapeDtypeStruct((rows, n * cols), jnp.bfloat16),
        input_output_aliases={} if out is None else {4: 0},
        cost_estimate=pl.CostEstimate(flops=6 * size * cols, bytes_accessed=4 * size * cols, transcendentals=0),
    )(*operands)


def per_device(n, n_mp, activations, weight, thresholds):
    ids = np.arange(n)
    plan = [target(k, ids, n) for k in range(n)]
    me = lax.axis_index("dp")
    cols = weight.shape[1]
    rows = weight.shape[0] // n
    total_cols = cols * n * n_mp

    pieces = pieces_of(n, rows)

    def send(x, step):
        return lax.ppermute(x, "dp", [(i, int(plan[step][i])) for i in range(n)])

    def take(rest, step, top, size):
        return lax.dynamic_slice(rest, (target(step, me, n, jnp.where) * rows + top, 0), (size, cols))

    blocks, rest = [], weight
    for i, piece in enumerate(pieces):
        ahead = i < 2 and cols % 128 == 0 and rows % 512 == 0
        blocks.append(take_ahead(rest, *piece, n, rows) if ahead else take(rest, *piece))
        if i < 2:
            rest, _ = lax.optimization_barrier((rest, blocks[-1]))
    arrived = [send(block, step) for block, (step, _, _) in zip(blocks, pieces)]

    partial_value = jnp.sum(jnp.square(activations.astype(jnp.float32)), axis=0)
    squares = gather_sums(partial_value.reshape(n, cols), n)
    col_norm = jnp.sqrt(squares)
    row_part = jnp.sum(jnp.abs(weight.astype(jnp.float32)) * col_norm[None, :], axis=1).reshape(n, rows)
    row_part, norms = gather_sums(row_part, n, col_norm)
    by_step = np.stack([source(k, ids, n) for k in range(n)], 1)
    by_step = by_step % group_size(n) * (n // group_size(n)) + by_step // group_size(n)
    by_step = lax.dynamic_index_in_dim(jnp.asarray(by_step.astype(np.int32)), me, 0, keepdims=False)
    norms = jnp.take(norms, by_step, axis=0, mode="clip")
    row_total = lax.psum(row_part, "mp")
    row_mean = row_total / total_cols + small_eps
    slope = (gate_slope / row_mean)[:, None]
    shift = (0.5 - gate_slope * thresholds)[:, None]

    late = [i for i, (step, _, _) in enumerate(pieces) if 5 * n // 16 <= step < n // 2]
    order = [i for i in range(len(pieces)) if i not in late] + late
    if cols % 128 == 0 and rows % 128 == 0:
        norms, slope, shift = [pltpu.with_memory_space_constraint(v, pltpu.VMEM) for v in (norms, slope, shift)]
        out = None
        for i in order:
            step, top, _ = pieces[i]
            near = i in order[-2:]
            out = prune_block(arrived[i], norms, slope, shift, step, top, n, out, near)
        return out
    out = jnp.zeros((rows, n * cols), jnp.bfloat16)
    for i in order:
        step, top, size = pieces[i]
        wide = arrived[i].astype(jnp.float32)
        ours = slice(top, top + size)
        owner = source(step, me, n, jnp.where)
        share = jnp.clip(jnp.abs(wide) * norms[step] * slope[ours] + shift[ours], 0.0, 1.0)
        out = lax.dynamic_update_slice(out, (wide * share).astype(jnp.bfloat16), (top, owner * cols))
    return out


def solution(mesh):
    placed = (P("dp", "mp"), P(None, ("mp", "dp")), P("dp"))
    n, n_mp = mesh.shape["dp"], mesh.shape["mp"]
    return jax.shard_map(
        functools.partial(per_device, n, n_mp),
        mesh=mesh,
        in_specs=placed,
        out_specs=P("dp", "mp"),
        check_vma=False,
    )
```
